256 devices in a mesh: space: 64 (over z, x, core), member: 4 (over y).
Axes of the slice: x: 4, y: 4, z: 8, core: 2. Of those that a mesh axis runs over, the one named last changes fastest.
Arguments:
- head_start: float32 [32, 4, 2048, 256], P('member', None, 'space'), parts along dimension 0, may hold values from -4 to 4
- recharge: float32 [32, 2048, 256], P('member', 'space'), parts along dimension 0, may hold values from -3 to 3
- section_start: float32 [32, 65536], P('member', 'space'), parts along dimension 0, may hold values from -4 to 4
- inflow: float32 [32, 65536], P('member', 'space'), parts along dimension 0, may hold values from -4 to 4
- soil_class: int32 [4, 2048, 256], P(None, 'space'), may hold values from 0 to 11
- class_conduct: float32 [12], replicated, may hold values from 0.5 to 4
- class_alpha: float32 [12], replicated, may hold values from 0.3 to 2
- capacity: float32 [4, 2048, 256], P(None, 'space'), may hold values from 0.5 to 2
- river_cell: int32 [64, 6, 512], P('space'), may hold values from -1 to 8191, as said below
- river_reach: int32 [64, 6, 512], P('space'), may hold values from -1 to 1023, as said below
- river_cond: float32 [64, 6, 512], P('space'), may hold values from 0.5 to 2
- reach_rate: float32 [65536], P('space'), may hold values from 0.2 to 1
Outputs:
- water_head: float32 [32, 4, 2048, 256], P('member', None, 'space'), parts along dimension 0
- reach_section: float32 [32, 65536], P('member', 'space'), parts along dimension 0
The draws below stay inside these ranges and needn't reach their ends.
There are 4 independent parts, one for each index of `member`. The reference program is written for one: setup_inputs(seed, part) draws one part's arguments, and reference() takes and returns one part's arrays. A program takes and returns all parts, laid end to end along the dimension named above; an argument that names none is the same for every part. Nothing has to cross between parts.
Inputs may be any that keep to these rules, and one draw needn't show every extreme that they name: `river_reach`: -1 marks an empty slot. Otherwise slot j of bucket b of tile t names a reach of that bucket's owner, which lies on the grid. The live slots of a bucket come first. Every tile has a bucket with all 512 slots live, and in every draw all buckets aimed at some one tile are full. `river_cell`: -1 exactly where river_reach is -1; otherwise a top-layer column x * 256 + y with x counted within the tile. A column may carry several slots.
All inputs are finite; a program needn't handle non-finite values.
Results may differ from the reference program's by a relative error of at most 0.00002.
Values sent between devices are 32-bit elements; how exact they have to be, the bound alone decides.
A program may use at most 64 MiB of HBM per device.

```python
import math
import jax
import jax.numpy as jnp

MEMBERS = 8
LAYERS = 4
CX = 32
NY = 256
R_DEV = 1024
SLOT = 512
SPAN = 2
BUCKETS = 6
CLASSES = 12
PICARD = 2
SWEEPS = 3
NX = 2048
REACHES = 65536
N_SPACE = 64


def river_layout(key):
    base = jax.random.fold_in(key, 31)
    keys = jax.random.split(base, 5)
    bucket_count = 2 * SPAN + 2
    tiles = jnp.arange(N_SPACE, dtype=jnp.int32)[:, None]
    offsets = jnp.arange(bucket_count, dtype=jnp.int32)[None, :]
    owner = jnp.where(offsets == bucket_count - 1, (tiles + N_SPACE // 2) % N_SPACE, tiles + offsets - SPAN)
    inside = (owner >= 0) & (owner < N_SPACE)
    counts = jax.random.randint(keys[0], (N_SPACE, bucket_count), SLOT // 2, SLOT + 1)
    target = jax.random.randint(keys[1], (), 0, N_SPACE)
    chosen = jax.random.randint(keys[2], (N_SPACE, 1), 0, 2 * SPAN + 1)
    chosen = jnp.clip(chosen, SPAN - tiles, SPAN + N_SPACE - 1 - tiles)
    filled = (owner == target) | (offsets == chosen)
    counts = jnp.where(filled, SLOT, counts)
    counts = jnp.where(inside, counts, 0)
    used = jnp.arange(SLOT, dtype=jnp.int32)[None, None, :] < counts[:, :, None]
    reaches = jax.random.randint(keys[3], (N_SPACE, bucket_count, SLOT), 0, R_DEV)
    columns = jax.random.randint(keys[4], (N_SPACE, bucket_count, SLOT), 0, CX * NY)
    return (jnp.where(used, reaches, -1), jnp.where(used, columns, -1))


def draw_river_reach(key, part):
    return river_layout(key)[0].astype(jnp.int32)


def draw_river_cell(key, part):
    return river_layout(key)[1].astype(jnp.int32)


def with_ends(values, rng, smallest, largest):
    dims = values.shape
    spot = [jax.random.randint(jax.random.fold_in(rng, axis), (), 0, dims[axis]) for axis in range(len(dims))]
    values = values.at[tuple(spot)].set(smallest)
    longest = dims.index(max(dims))
    spot[longest] = (spot[longest] + 1) % dims[longest]
    return values.at[tuple(spot)].set(largest)


def steps_of(own_key, shape, pieces, least, high):
    level, own = 1.0, jax.random.fold_in(own_key, 6)
    for position, shards_of in pieces:
        steps = jnp.exp(jax.random.uniform(jax.random.fold_in(own, position), (shards_of,), jnp.float32, least / len(pieces), high / len(pieces)))
        level = level * jnp.repeat(steps, shape[position] // shards_of).reshape([-1 if axis == position else 1 for axis in range(len(shape))])
    return level


def gaussian(own_key, extent, scale, limit, shards=(), kind=jnp.bfloat16):
    result = jax.random.normal(own_key, extent, jnp.float32) * scale
    if len(shards) > 0:
        result = steps_of(own_key, extent, shards, -0.22, 0.18) * result
    return jnp.clip(result, min=-limit, max=limit).astype(kind)


def setup_inputs(seed: int = 0, part: int = 0) -> dict:
    key_list = jax.random.split(jax.random.key(seed), 13)
    part_splits = jax.random.split(jax.random.fold_in(key_list[12], part), 13)
    return {
        "head_start": gaussian(part_splits[0], (MEMBERS, LAYERS, NX, NY), 1.0, 4.0, ((2, 64),), jnp.float32),
        "recharge": gaussian(part_splits[1], (MEMBERS, NX, NY), 0.5, 3.0, ((1, 64),), jnp.float32),
        "section_start": gaussian(part_splits[2], (MEMBERS, REACHES), 1.0, 4.0, ((1, 64),), jnp.float32),
        "inflow": gaussian(part_splits[3], (MEMBERS, REACHES), 1.0, 4.0, ((1, 64),), jnp.float32),
        "soil_class": with_ends(jax.random.randint(key_list[4], (LAYERS, NX, NY), 0, CLASSES), jax.random.fold_in(key_list[4], 1), 0, CLASSES - 1).astype(jnp.int32),
        "class_conduct": jnp.clip(jnp.exp(jax.random.uniform(key_list[5], (CLASSES,), jnp.float32, math.log(0.5), math.log(4.0))), 0.5, 4.0),
        "class_alpha": jnp.clip(jnp.exp(jax.random.uniform(key_list[6], (CLASSES,), jnp.float32, math.log(0.3), math.log(2.0))), 0.3, 2.0),
        "capacity": jnp.clip(jnp.exp(math.log(2.0) - 1.3862944 * jax.random.uniform(key_list[7], (LAYERS, NX, NY), jnp.float32) ** steps_of(key_list[7], (LAYERS, NX, NY), ((1, 64),), -0.2, 0.2)), 0.5, 2.0),
        "river_cell": draw_river_cell(jax.random.fold_in(key_list[12], 71), part),
        "river_reach": draw_river_reach(jax.random.fold_in(key_list[12], 71), part),
        "river_cond": jnp.clip(jnp.exp(math.log(2.0) - 1.3862944 * jax.random.uniform(key_list[10], (N_SPACE, BUCKETS, SLOT), jnp.float32) ** steps_of(key_list[10], (N_SPACE, BUCKETS, SLOT), ((0, 64),), -0.2, 0.2)), 0.5, 2.0),
        "reach_rate": jnp.clip(jnp.exp(math.log(1.0) - 1.609438 * jax.random.uniform(key_list[11], (REACHES,), jnp.float32) ** steps_of(key_list[11], (REACHES,), ((0, 64),), -0.2, 0.2)), 0.2, 1.0),
    }


vertical_ratio = 0.5


def harmonic(first, second):
    return 2.0 * first * second / (first + second)


def faces(conduct):
    along_x = jnp.pad(conduct, ((0, 0), (0, 0), (1, 1), (0, 0)))
    along_y = jnp.pad(conduct, ((0, 0), (0, 0), (0, 0), (1, 1)))
    along_z = jnp.pad(conduct, ((0, 0), (1, 1), (0, 0), (0, 0)))
    return (harmonic(conduct, along_x[:, :, 2:]), harmonic(conduct, along_x[:, :, :-2]),
            harmonic(conduct, along_y[..., 2:]), harmonic(conduct, along_y[..., :-2]),
            vertical_ratio * harmonic(conduct, along_z[:, 2:]),
            vertical_ratio * harmonic(conduct, along_z[:, :-2]))


def relax(head_now, source_term, diagonal, links):
    along_x = jnp.pad(head_now, ((0, 0), (0, 0), (1, 1), (0, 0)))
    along_y = jnp.pad(head_now, ((0, 0), (0, 0), (0, 0), (1, 1)))
    along_z = jnp.pad(head_now, ((0, 0), (1, 1), (0, 0), (0, 0)))
    total = source_term + links[0] * along_x[:, :, 2:] + links[1] * along_x[:, :, :-2]
    total = total + links[2] * along_y[..., 2:] + links[3] * along_y[..., :-2]
    total = total + links[4] * along_z[:, 2:] + links[5] * along_z[:, :-2]
    return total / diagonal


def reference(head_start, recharge, section_start, inflow, soil_class, class_conduct, class_alpha, capacity, river_cell, river_reach, river_cond, reach_rate):
    members = head_start.shape[0]
    cell_conduct = class_conduct[soil_class]
    cell_alpha = class_alpha[soil_class]
    tiles = jnp.arange(N_SPACE, dtype=jnp.int32)[:, None, None]
    offsets = jnp.arange(2 * SPAN + 2, dtype=jnp.int32)[None, :, None]
    owner = jnp.where(offsets == 2 * SPAN + 1, (tiles + N_SPACE // 2) % N_SPACE, tiles + offsets - SPAN).astype(jnp.int32)
    live_slot = river_reach >= 0
    target = jnp.where(live_slot, owner * R_DEV + river_reach, 0).reshape(-1).astype(jnp.int32)
    column = jnp.where(live_slot, tiles * (CX * NY) + river_cell, 0).reshape(-1).astype(jnp.int32)
    weight = jnp.where(live_slot, river_cond, jnp.float32(0.0)).reshape(-1)
    col_cond = jnp.zeros((NX * NY,), jnp.float32).at[column].add(weight).reshape(NX, NY)
    section_now = section_start
    head_now = head_start
    for outer in range(PICARD):
        fetched = section_now[:, target]
        river_rhs = jnp.zeros((members, NX * NY), jnp.float32).at[:, column].add(weight[None] * fetched)
        river_rhs = river_rhs.reshape(members, NX, NY)
        conduct = cell_conduct * jnp.exp(cell_alpha * jnp.minimum(head_now, 0.0))
        links = faces(conduct)
        diagonal = capacity + links[0] + links[1] + links[2] + links[3] + links[4] + links[5]
        diagonal = diagonal.at[:, 0].add(col_cond)
        source_term = capacity * head_start
        source_term = source_term.at[:, 0].add(recharge + river_rhs)
        for sweep in range(SWEEPS):
            head_now = relax(head_now, source_term, diagonal, links)
        top_head = head_now[:, 0].reshape(members, -1)[:, column]
        leakage = weight[None] * (fetched - top_head)
        reach_leak = jnp.zeros((members, N_SPACE * R_DEV), jnp.float32).at[:, target].add(leakage)
        section_now = section_start + reach_rate[None] * (inflow - reach_leak)
    return head_now, section_now
```

```python
import functools

import jax
import jax.numpy as jnp
from jax import lax
from jax.experimental import pallas as pl
from jax.experimental.pallas import tpu as pltpu
from jax.sharding import PartitionSpec as P

PICARD = 2
SWEEPS = 3
NEAR = 2
FAR = 2 * NEAR + 1
LANES = 128
F32 = jnp.float32
BF16 = jnp.bfloat16


def harmonic(first, second):
    return 2.0 * first * second / (first + second)


def halves(values):
    high = values.astype(BF16)
    return high, (values - high.astype(F32)).astype(BF16)


def dot_rows(left, right):
    return lax.dot_general(left, right, (((1,), (1,)), ((), ())), preferred_element_type=F32)


def kernel(
    tile_count,
    head_in, recharge_in, section_in, inflow_in, soil_in, class_conduct, class_alpha,
    capacity_in, cell_in, reach_in, cond_in, rate_in,
    head_out, section_out,
    stage, recharge, section, inflow, soil, capacity, cell, reach, cond, rate,
    heads, kc, ka, base, source, face_x, face_y, face_z, inverse, col_cond,
    one_y, mask_x, one_r, weight, fetched, leak, river,
    edge, edge_got, sect0, sect1, part1, part2, got1, got2, partial_state, state_got, rate_got,
    load_sem, store_sem, halo_send, halo_recv, edge_send, edge_recv,
    sect_send, sect_recv, leak_send, leak_recv, state_send, state_recv, rate_send, rate_recv,
):
    me = lax.axis_index("space")
    layers, padded, members, width = heads.shape[1:]
    rows = padded - 2
    buckets, slots = cell.shape
    groups = section.shape[1] // LANES
    near = [bucket for bucket in range(buckets) if bucket not in (NEAR, FAR)]
    remote = near + [FAR]

    def tile(shift):
        return lax.rem(me + shift + tile_count, tile_count)

    def user(bucket):
        return tile(tile_count // 2 if bucket == FAR else NEAR - bucket)

    def owner(bucket):
        return tile(tile_count // 2 if bucket == FAR else bucket - NEAR)

    def send(source_ref, target_ref, send_sem, recv_sem, device):
        return pltpu.make_async_remote_copy(
            src_ref=source_ref, dst_ref=target_ref, send_sem=send_sem, recv_sem=recv_sem,
            device_id={"space": device}, device_id_type=pl.DeviceIdType.MESH)

    loads = {}
    pairs = [("section", section_in, section), ("rate", rate_in, rate), ("soil", soil_in, soil)]
    for half in range(2):
        lanes = pl.ds(half * LANES, LANES)
        pairs.append(("head%d" % half, head_in.at[:, lanes], stage.at[half]))
        pairs.append(("recharge%d" % half, recharge_in.at[:, lanes], recharge.at[half]))
    pairs += [("capacity", capacity_in, capacity), ("cell", cell_in, cell), ("reach", reach_in, reach),
              ("cond", cond_in, cond), ("inflow", inflow_in, inflow)]
    for index, (name, source_ref, target_ref) in enumerate(pairs):
        loads[name] = pltpu.make_async_copy(source_ref, target_ref, load_sem.at[index])
        loads[name].start()

    barrier = pltpu.get_barrier_semaphore()
    for bucket in remote:
        pl.semaphore_signal(barrier, inc=1, device_id={"space": user(bucket)},
                            device_id_type=pl.DeviceIdType.MESH)
    pl.semaphore_wait(barrier, len(remote))

    sends = []
    loads["section"].wait()
    loads["rate"].wait()
    first_sections = {}
    for bucket in [FAR] + near:
        copy = send(section, sect0.at[bucket], sect_send.at[0, bucket], sect_recv.at[0, bucket], user(bucket))
        copy.start()
        first_sections[bucket] = copy
        sends.append(copy)
    rate_copy = send(rate, rate_got, rate_send, rate_recv, user(FAR))
    rate_copy.start()
    sends.append(rate_copy)

    loads["soil"].wait()
    classes = soil[...]
    conduct_of = jnp.zeros(classes.shape, F32)
    alpha_of = jnp.zeros(classes.shape, F32)
    for index in range(class_conduct.shape[0]):
        match = classes == index
        conduct_of = jnp.where(match, class_conduct[index], conduct_of)
        alpha_of = jnp.where(match, class_alpha[index], alpha_of)
    kc[:, 1:rows + 1, :] = conduct_of
    ka[:, 1:rows + 1, :] = alpha_of
    for side, row in ((0, 0), (1, rows - 1)):
        for layer in range(layers):
            edge[side, layer:layer + 1, :] = conduct_of[layer, row:row + 1, :]
            edge[side, layers + layer:layers + layer + 1, :] = alpha_of[layer, row:row + 1, :]
    edge_copies = []
    for side, shift in ((0, -1), (1, 1)):
        copy = send(edge.at[side], edge_got.at[1 - side], edge_send.at[side], edge_recv.at[1 - side], tile(shift))
        copy.start()
        edge_copies.append(copy)
        sends.append(copy)

    def halo(index):
        copies = [
            send(heads.at[index, :, 1], heads.at[index, :, rows + 1],
                 halo_send.at[index, 0], halo_recv.at[index, 1], tile(-1)),
            send(heads.at[index, :, rows], heads.at[index, :, 0],
                 halo_send.at[index, 1], halo_recv.at[index, 0], tile(1)),
        ]
        for copy in copies:
            copy.start()
        sends.extend(copies)
        return copies

    for half in range(2):
        loads["head%d" % half].wait()
        loads["recharge%d" % half].wait()
    loads["capacity"].wait()

    def begin(x):
        for layer in range(layers):
            cap = capacity[layer, pl.ds(x, 1), :]
            for half in range(2):
                lanes = slice(half * LANES, (half + 1) * LANES)
                value = stage[half, pl.ds(layer * rows + x, members, stride=layers * rows), :]
                heads[0, layer, x + 1, :, lanes] = value
                term = cap[:, lanes] * value
                if layer == 0:
                    term = term + recharge[half, pl.ds(x, members, stride=rows), :]
                base[layer, x, :, lanes] = term

    def over(start, stop, body):
        def step(x, carry):
            body(x)
            return carry
        lax.fori_loop(start, stop, step, 0)

    begin(0)
    begin(rows - 1)
    halos = halo(0)
    over(1, rows - 1, begin)

    loads["cell"].wait()
    loads["reach"].wait()
    loads["cond"].wait()
    live = reach[...] >= 0
    columns = jnp.where(live, cell[...], 0)
    reaches = jnp.where(live, reach[...], 0)
    weight[...] = jnp.where(live, cond[...], 0.0)
    column_x = columns // width
    column_y = columns % width
    reach_high = reaches // LANES
    reach_low = reaches % LANES
    ids = lax.broadcasted_iota(jnp.int32, (width, slots), 0)
    total = jnp.zeros((2 * rows, width), F32)
    for bucket in range(buckets):
        own = slice(bucket, bucket + 1)
        one_y[bucket] = (ids == column_y[own]).astype(F32).astype(BF16)
        mask_x[bucket] = (ids // members == column_x[own]).astype(F32).astype(BF16)
        one_r[bucket] = (ids % LANES == reach_low[own]).astype(F32).astype(BF16)
        terms = jnp.where(ids[:rows] == column_x[own], weight[own, :], 0.0)
        total = total + dot_rows(jnp.concatenate(halves(terms), axis=0), one_y[bucket])
    col_cond[...] = total[:rows] + total[rows:]

    for copy in edge_copies:
        copy.wait_recv()
    for side, row, outside in ((0, 0, 0), (1, rows + 1, tile_count - 1)):
        inside = jnp.where(me == outside, 0.0, 1.0)
        for layer in range(layers):
            kc[layer, row:row + 1, :] = edge_got[side, layer:layer + 1, :] * inside
            ka[layer, row:row + 1, :] = edge_got[side, layers + layer:layers + layer + 1, :]

    lane = lax.broadcasted_iota(jnp.int32, (members, width), 1)

    def conduct(index, x):
        return tuple(
            kc[layer, pl.ds(x, 1), :]
            * jnp.exp(ka[layer, pl.ds(x, 1), :] * jnp.minimum(heads[index, layer, x], 0.0))
            for layer in range(layers))

    def link(index):
        low = conduct(index, 0)
        here = conduct(index, 1)
        before = tuple(harmonic(a, b) for a, b in zip(low, here))
        for layer in range(layers):
            face_x[layer, 0] = before[layer]

        def step(x, carry):
            here, before = carry
            after = conduct(index, x + 1)
            ahead = tuple(harmonic(a, b) for a, b in zip(here, after))
            down = None
            for layer in range(layers):
                face_x[layer, x] = ahead[layer]
                along = harmonic(here[layer], pltpu.roll(here[layer], width - 1, 1))
                along = jnp.where(lane == width - 1, 0.0, along)
                face_y[layer, x - 1] = along
                diagonal = capacity[layer, pl.ds(x - 1, 1), :] + ahead[layer] + before[layer]
                diagonal = diagonal + along + pltpu.roll(along, 1, 1)
                if layer > 0:
                    diagonal = diagonal + down
                if layer < layers - 1:
                    down = 0.5 * harmonic(here[layer], here[layer + 1])
                    face_z[layer, x - 1] = down
                    diagonal = diagonal + down
                if layer == 0:
                    diagonal = diagonal + col_cond[pl.ds(x - 1, 1), :]
                inverse[layer, x - 1] = 1.0 / diagonal
            return after, ahead

        lax.fori_loop(1, rows + 1, step, (here, before))

    def relax(index, x):
        now = [heads[index, layer, x] for layer in range(layers)]
        results = []
        for layer in range(layers):
            along = face_y[layer, x - 1]
            total = source[x - 1] if layer == 0 else base[layer, x - 1]
            total = total + face_x[layer, x] * heads[index, layer, x + 1]
            total = total + face_x[layer, x - 1] * heads[index, layer, x - 1]
            total = total + along * pltpu.roll(now[layer], width - 1, 1)
            total = total + pltpu.roll(along * now[layer], 1, 1)
            if layer < layers - 1:
                total = total + face_z[layer, x - 1] * now[layer + 1]
            if layer > 0:
                total = total + face_z[layer - 1, x - 1] * now[layer - 1]
            results.append(total * inverse[layer, x - 1])
        return results

    def sweep(index, last):
        def body(x):
            results = relax(index, x)
            for layer in range(layers):
                if layer == 0 or not last:
                    heads[index + 1, layer, x] = results[layer]
                if last:
                    for half in range(2):
                        stage[half, pl.ds(layer * rows + x - 1, members, stride=layers * rows), :] = (
                            results[layer][:, half * LANES:(half + 1) * LANES])
        if last:
            over(1, rows + 1, body)
            return None
        body(1)
        body(rows)
        copies = halo(index + 1)
        over(2, rows, body)
        return copies

    def by_group(values):
        return jnp.concatenate([values[:, g * LANES:(g + 1) * LANES] for g in range(groups)], axis=0)

    def river_term(sections):
        total = jnp.zeros((2 * rows * members, width), F32)
        for bucket in [NEAR] + remote:
            own = slice(bucket, bucket + 1)
            left = jnp.concatenate(halves(by_group(sections(bucket))), axis=1)
            picked = jnp.dot(left, one_r[bucket], preferred_element_type=F32)
            value = jnp.zeros((members, slots), F32)
            for g in range(groups):
                value = value + jnp.where(reach_high[own] == g, picked[g * members:(g + 1) * members], 0.0)
            fetched[bucket] = value
            flow = weight[own, :] * value
            terms = halves(jnp.concatenate([flow, flow], axis=0))
            spread = [mask_x[bucket] * jnp.concatenate([term] * (rows // 2), axis=0) for term in terms]
            total = total + dot_rows(jnp.concatenate(spread, axis=0), one_y[bucket])
        river[...] = (total[:rows * members] + total[rows * members:]).reshape(rows, members, width)

    def leak_parts(index, parts):
        top = heads[index, 0, 1:rows + 1].reshape(rows * members, width)
        terms = halves(top)
        for bucket in [FAR] + near + [NEAR]:
            own = slice(bucket, bucket + 1)
            picked = jnp.dot(terms[0], one_y[bucket], preferred_element_type=F32)
            picked = picked + jnp.dot(terms[1], one_y[bucket], preferred_element_type=F32)
            value = jnp.zeros((members, slots), F32)
            for x in range(rows):
                value = value + jnp.where(column_x[own] == x, picked[x * members:(x + 1) * members], 0.0)
            flow = weight[own, :] * (fetched[bucket] - value)
            spread = jnp.concatenate([jnp.where(reach_high[own] == g, flow, 0.0) for g in range(groups)], axis=0)
            sums = dot_rows(jnp.concatenate(halves(spread), axis=0), one_r[bucket, :LANES, :])
            sums = sums[:groups * members] + sums[groups * members:]
            for g in range(groups):
                parts[bucket, :, g * LANES:(g + 1) * LANES] = sums[g * members:(g + 1) * members]

    def send_parts(step, parts, got):
        copies = {}
        for bucket in [FAR] + near:
            copy = send(parts.at[bucket], got.at[bucket], leak_send.at[step, bucket],
                        leak_recv.at[step, bucket], owner(bucket))
            copy.start()
            copies[bucket] = copy
            sends.append(copy)
        return copies

    def near_state(parts, got):
        values = parts[NEAR]
        for bucket in near:
            values = values + got[bucket]
        return values

    def with_rate(rates, values):
        return jnp.concatenate(
            [rates[g:g + 1, :] * values[:, g * LANES:(g + 1) * LANES] for g in range(groups)], axis=1)

    for copy in halos:
        copy.wait_recv()
    link(0)
    for bucket in [FAR] + near:
        first_sections[bucket].wait_recv()
    river_term(lambda bucket: section[...] if bucket == NEAR else sect0[bucket])
    source[...] = base[0] + river[...]
    index = 0
    for sweep_index in range(SWEEPS):
        if sweep_index > 0:
            for copy in halos:
                copy.wait_recv()
        halos = sweep(index, False)
        index += 1
    leak_parts(index, part1)
    copies = send_parts(0, part1, got1)
    for copy in halos:
        copy.wait_recv()
    link(index)

    loads["inflow"].wait()
    rate_copy.wait_recv()
    for bucket in near:
        copies[bucket].wait_recv()
    partial_state[...] = section[...] + with_rate(rate, inflow[...] - near_state(part1, got1))
    state_copy = send(partial_state, state_got, state_send, state_recv, user(FAR))
    state_copy.start()
    sends.append(state_copy)
    copies[FAR].wait_recv()
    sect1[NEAR] = partial_state[...] - with_rate(rate, got1[FAR])
    second_sections = []
    for bucket in near:
        copy = send(sect1.at[NEAR], sect1.at[bucket], sect_send.at[1, bucket], sect_recv.at[1, bucket], user(bucket))
        copy.start()
        second_sections.append(copy)
        sends.append(copy)
    state_copy.wait_recv()
    sect1[FAR] = state_got[...] - with_rate(rate_got, part1[FAR])
    for copy in second_sections:
        copy.wait_recv()

    river_term(lambda bucket: sect1[bucket])
    source[...] = base[0] + river[...]
    for sweep_index in range(SWEEPS):
        if sweep_index > 0:
            for copy in halos:
                copy.wait_recv()
        halos = sweep(index, sweep_index == SWEEPS - 1)
        index += 1
    stores = []
    for half in range(2):
        copy = pltpu.make_async_copy(stage.at[half], head_out.at[:, pl.ds(half * LANES, LANES)], store_sem.at[half])
        copy.start()
        stores.append(copy)
    leak_parts(index, part2)
    copies = send_parts(1, part2, got2)
    for bucket in remote:
        copies[bucket].wait_recv()
    values = near_state(part2, got2) + got2[FAR]
    leak[...] = section[...] + with_rate(rate, inflow[...] - values)
    copy = pltpu.make_async_copy(leak, section_out, store_sem.at[2])
    copy.start()
    stores.append(copy)
    for copy in stores:
        copy.wait()
    for copy in sends:
        copy.wait_send()


def body(tile_count, head_start, recharge, section_start, inflow, soil_class, class_conduct, class_alpha,
         capacity, river_cell, river_reach, river_cond, reach_rate):
    members, layers, rows, width = head_start.shape
    buckets, slots = river_cell.shape[1:]
    reaches = section_start.shape[1]
    groups = reaches // LANES
    any_spec = pl.BlockSpec(memory_space=pl.ANY)
    smem_spec = pl.BlockSpec(memory_space=pltpu.SMEM)
    vmem = pltpu.VMEM
    grid = (layers, rows, members, width)
    state = (members, reaches)
    scratch = [
        vmem((2, members * layers * rows, LANES), F32), vmem((2, members * rows, LANES), F32),
        vmem(state, F32), vmem(state, F32), vmem((layers, rows, width), jnp.int32), vmem((layers, rows, width), F32),
        vmem((buckets, slots), jnp.int32), vmem((buckets, slots), jnp.int32), vmem((buckets, slots), F32),
        vmem((groups, LANES), F32),
        vmem((PICARD * SWEEPS + 1, layers, rows + 2, members, width), F32),
        vmem((layers, rows + 8, width), F32), vmem((layers, rows + 8, width), F32),
        vmem(grid, F32), vmem((rows, members, width), F32),
        vmem((layers, rows + 1, members, width), F32), vmem(grid, F32),
        vmem((layers - 1, rows, members, width), F32), vmem(grid, F32), vmem((rows, width), F32),
        vmem((buckets, width, slots), BF16), vmem((buckets, rows * members, slots), BF16),
        vmem((buckets, 2 * LANES, slots), BF16),
        vmem((buckets, slots), F32), vmem((buckets, members, slots), F32), vmem(state, F32),
        vmem((rows, members, width), F32),
        vmem((2, 2 * layers, width), F32), vmem((2, 2 * layers, width), F32),
    ] + [vmem((buckets,) + state, F32)] * 6 + [vmem(state, F32)] * 2 + [vmem((groups, LANES), F32)] + [
        pltpu.SemaphoreType.DMA((12,)), pltpu.SemaphoreType.DMA((3,)),
        pltpu.SemaphoreType.DMA((PICARD * SWEEPS, 2)), pltpu.SemaphoreType.DMA((PICARD * SWEEPS, 2)),
        pltpu.SemaphoreType.DMA((2,)), pltpu.SemaphoreType.DMA((2,)),
        pltpu.SemaphoreType.DMA((2, buckets)), pltpu.SemaphoreType.DMA((2, buckets)),
        pltpu.SemaphoreType.DMA((2, buckets)), pltpu.SemaphoreType.DMA((2, buckets)),
        pltpu.SemaphoreType.DMA, pltpu.SemaphoreType.DMA, pltpu.SemaphoreType.DMA, pltpu.SemaphoreType.DMA,
    ]
    head, section = pl.pallas_call(
        functools.partial(kernel, tile_count),
        out_shape=(jax.ShapeDtypeStruct((members * layers * rows, width), F32),
                   jax.ShapeDtypeStruct(state, F32)),
        in_specs=[any_spec] * 5 + [smem_spec] * 2 + [any_spec] * 5,
        out_specs=(any_spec, any_spec),
        scratch_shapes=scratch,
        compiler_params=pltpu.CompilerParams(
            collective_id=0, has_side_effects=True, vmem_limit_bytes=60 * 1024 * 1024),
        name="aquifer",
    )(head_start.reshape(-1, width), recharge.reshape(-1, width), section_start, inflow, soil_class,
      class_conduct, class_alpha, capacity, river_cell[0], river_reach[0], river_cond[0],
      reach_rate.reshape(groups, LANES))
    return head.reshape(head_start.shape), section


def solution(mesh):
    return jax.shard_map(
        functools.partial(body, mesh.shape["space"]),
        mesh=mesh,
        in_specs=(
            P("member", None, "space", None),
            P("member", "space", None),
            P("member", "space"),
            P("member", "space"),
            P(None, "space", None),
            P(),
            P(),
            P(None, "space", None),
            P("space", None, None),
            P("space", None, None),
            P("space", None, None),
            P("space"),
        ),
        out_specs=(P("member", None, "space", None), P("member", "space")),
        check_vma=False,
    )
```

```python
import functools

import jax
import jax.numpy as jnp
from jax import lax
from jax.experimental import pallas as pl
from jax.experimental.pallas import tpu as pltpu
from jax.sharding import PartitionSpec as P

PICARD = 2
SWEEPS = 3
NEAR = 2
FAR = 2 * NEAR + 1
LANES = 128
F32 = jnp.float32
BF16 = jnp.bfloat16


def halves(values):
    high = values.astype(BF16)
    return high, (values - high.astype(F32)).astype(BF16)


def dot_rows(left, right):
    return lax.dot_general(left, right, (((1,), (1,)), ((), ())), preferred_element_type=F32)


def kernel(
    tile_count,
    head_in, recharge_in, section_in, inflow_in, soil_in, class_conduct, class_alpha,
    capacity_in, cell_in, reach_in, cond_in, rate_in,
    head_out, section_out,
    head0, head1, head2, head3, head4, head5, head6,
    recharge, section, inflow, soil, capacity, cell, reach, cond, rate,
    kc, ka, base, source, face_x, face_y, face_z, inverse, col_cond,
    one_y, mask_x, one_r, spread, weight, column_x, column_y, reach_high, reach_low, fetched, river,
    edge, edge_got, sect0, sect1, part1, part2, got1, got2, partial_state, state_got, rate_got,
    load_sem, head_sem, recharge_sem, store_sem, halo_send, halo_recv, edge_send, edge_recv,
    sect_send, sect_recv, leak_send, leak_recv, state_send, state_recv, rate_send, rate_recv,
):
    me = lax.axis_index("space")
    heads = (head0, head1, head2, head3, head4, head5, head6)
    layers, padded, members, width = head0.shape
    rows = padded - 2
    buckets, slots = weight.shape
    pieces = slots // LANES
    groups = section.shape[1] // LANES
    near = [bucket for bucket in range(buckets) if bucket not in (NEAR, FAR)]
    remote = near + [FAR]

    def tile(shift):
        return lax.rem(me + shift + tile_count, tile_count)

    def user(bucket):
        return tile(tile_count // 2 if bucket == FAR else NEAR - bucket)

    def owner(bucket):
        return tile(tile_count // 2 if bucket == FAR else bucket - NEAR)

    def own(bucket):
        return slice(bucket, bucket + 1)

    def slot_range(bucket):
        return slice(bucket * slots, (bucket + 1) * slots)

    sends = []

    def send(source_ref, target_ref, send_sem, recv_sem, device):
        copy = pltpu.make_async_remote_copy(
            src_ref=source_ref, dst_ref=target_ref, send_sem=send_sem, recv_sem=recv_sem,
            device_id={"space": device}, device_id_type=pl.DeviceIdType.MESH)
        copy.start()
        sends.append(copy)
        return copy

    def over(start, stop, size, body):
        def step(count, carry):
            body([start + count * size + offset for offset in range(size)])
            return carry
        lax.fori_loop(0, (stop - start) // size, step, 0)

    loads = {}
    pairs = [("soil", soil_in, soil), ("section", section_in, section), ("rate", rate_in, rate),
             ("cell", cell_in, cell), ("reach", reach_in, reach), ("cond", cond_in, cond)]
    for index, (name, source_ref, target_ref) in enumerate(pairs):
        loads[name] = pltpu.make_async_copy(source_ref, target_ref, load_sem.at[index])
        loads[name].start()
    head_loads = [pltpu.make_async_copy(head_in.at[m], head0.at[:, 1:rows + 1, m, :], head_sem.at[m])
                  for m in range(members)]
    for copy in head_loads:
        copy.start()
    for index, (name, source_ref, target_ref) in enumerate(
            [("capacity", capacity_in, capacity), ("inflow", inflow_in, inflow)]):
        loads[name] = pltpu.make_async_copy(source_ref, target_ref, load_sem.at[len(pairs) + index])
        loads[name].start()
    recharge_loads = [pltpu.make_async_copy(recharge_in.at[m], recharge.at[:, m, :], recharge_sem.at[m])
                      for m in range(members)]
    for copy in recharge_loads:
        copy.start()

    barrier = pltpu.get_barrier_semaphore()
    for bucket in remote:
        pl.semaphore_signal(barrier, inc=1, device_id={"space": user(bucket)},
                            device_id_type=pl.DeviceIdType.MESH)

    loads["soil"].wait()
    classes = soil[...]
    conduct_of = jnp.zeros(classes.shape, F32)
    alpha_of = jnp.zeros(classes.shape, F32)
    for index in range(class_conduct.shape[0]):
        match = classes == index
        conduct_of = jnp.where(match, 2.0 * class_conduct[index], conduct_of)
        alpha_of = jnp.where(match, class_alpha[index], alpha_of)
    kc[:, 1:rows + 1, :] = conduct_of
    ka[:, 1:rows + 1, :] = alpha_of
    for side, row in ((0, 0), (1, rows - 1)):
        for layer in range(layers):
            edge[side, layer:layer + 1, :] = conduct_of[layer, row:row + 1, :]
            edge[side, layers + layer:layers + layer + 1, :] = alpha_of[layer, row:row + 1, :]

    loads["cell"].wait()
    loads["reach"].wait()
    loads["cond"].wait()
    live = reach[...] >= 0
    columns = jnp.where(live, cell[...], 0)
    reaches = jnp.where(live, reach[...], 0)
    for target_ref, values in (
            (weight, jnp.where(live, cond[...], 0.0)),
            (column_x, columns // width), (column_y, columns % width),
            (reach_high, reaches // LANES), (reach_low, reaches % LANES)):
        for bucket in range(buckets):
            for piece in range(pieces):
                line = bucket * pieces + piece
                target_ref[own(bucket), piece * LANES:(piece + 1) * LANES] = (
                    values[line:line + 1, :].astype(F32))

    def one_hot(ids, row):
        rows16 = jnp.broadcast_to(row, (16, slots)).astype(BF16)
        wide = jnp.concatenate([rows16] * (ids.shape[0] // 16), axis=0)
        return jnp.where(ids == wide, jnp.ones((), BF16), jnp.zeros((), BF16))

    ids = lax.broadcasted_iota(jnp.int32, (width, slots), 0)
    y_ids = ids.astype(F32).astype(BF16)
    x_ids = (ids // members).astype(F32).astype(BF16)
    r_ids = (ids % LANES).astype(F32).astype(BF16)

    def build(bucket):
        wide = slot_range(bucket)
        values = one_hot(y_ids, column_y[own(bucket), :])
        one_y[:width, wide] = values
        one_y[width:, wide] = values
        mask_x[:, wide] = one_hot(x_ids, column_x[own(bucket), :])
        one_r[:, wide] = one_hot(r_ids, reach_low[own(bucket), :])

    build(0)
    build(1)
    build(2)

    pl.semaphore_wait(barrier, len(remote))

    loads["section"].wait()
    loads["rate"].wait()
    first_sections = {}
    for bucket in [FAR] + near:
        first_sections[bucket] = send(
            section, sect0.at[bucket], sect_send.at[0, bucket], sect_recv.at[0, bucket], user(bucket))
    rate_copy = send(rate, rate_got, rate_send, rate_recv, user(FAR))
    edge_copies = [
        send(edge.at[side], edge_got.at[1 - side], edge_send.at[side], edge_recv.at[1 - side], tile(shift))
        for side, shift in ((0, -1), (1, 1))]

    def halo(index):
        return [
            send(heads[index].at[:, 1], heads[index].at[:, rows + 1],
                 halo_send.at[index, 0], halo_recv.at[index, 1], tile(-1)),
            send(heads[index].at[:, rows], heads[index].at[:, 0],
                 halo_send.at[index, 1], halo_recv.at[index, 0], tile(1)),
        ]

    for copy in head_loads:
        copy.wait()
    halos = halo(0)

    for bucket in range(3, buckets):
        build(bucket)
    flat = lax.broadcasted_iota(jnp.int32, (rows, slots), 0).astype(F32)
    total = jnp.zeros((2 * rows, width), F32)
    for bucket in range(buckets):
        terms = jnp.where(flat == column_x[own(bucket), :], weight[own(bucket), :], 0.0)
        total = total + dot_rows(jnp.concatenate(halves(terms), axis=0), one_y[:width, slot_range(bucket)])
    col_cond[...] = total[:rows] + total[rows:]

    loads["capacity"].wait()
    for copy in recharge_loads:
        copy.wait()

    def begin(block):
        for x in block:
            for layer in range(layers):
                term = capacity[layer, pl.ds(x, 1), :] * head0[layer, x + 1]
                base[layer, x] = term + recharge[x] if layer == 0 else term

    over(0, rows, 2, begin)

    for copy in edge_copies:
        copy.wait_recv()
    for side, row, outside in ((0, 0, 0), (1, rows + 1, tile_count - 1)):
        inside = jnp.where(me == outside, 0.0, 1.0)
        for layer in range(layers):
            kc[layer, row:row + 1, :] = edge_got[side, layer:layer + 1, :] * inside
            ka[layer, row:row + 1, :] = edge_got[side, layers + layer:layers + layer + 1, :]

    lane = lax.broadcasted_iota(jnp.int32, (members, width), 1)

    def harmonic(first, second):
        return first * second / (first + second)

    def conduct(head, x):
        return tuple(
            kc[layer, pl.ds(x, 1), :]
            * jnp.exp(ka[layer, pl.ds(x, 1), :] * jnp.minimum(head[layer, x], 0.0))
            for layer in range(layers))

    def link_start(head):
        low = conduct(head, 0)
        here = conduct(head, 1)
        before = tuple(harmonic(a, b) for a, b in zip(low, here))
        for layer in range(layers):
            face_x[layer, 0] = before[layer]
        return here, before

    def link(head, start, stop, carry):
        size = 2

        def step(count, carry):
            here, before = carry
            for offset in range(size):
                x = start + count * size + offset
                after = conduct(head, x + 1)
                ahead = tuple(harmonic(a, b) for a, b in zip(here, after))
                down = None
                for layer in range(layers):
                    face_x[layer, x] = ahead[layer]
                    along = harmonic(here[layer], pltpu.roll(here[layer], width - 1, 1))
                    along = jnp.where(lane == width - 1, 0.0, along)
                    face_y[layer, x - 1] = along
                    diagonal = capacity[layer, pl.ds(x - 1, 1), :] + ahead[layer] + before[layer]
                    diagonal = diagonal + along + pltpu.roll(along, 1, 1)
                    if layer > 0:
                        diagonal = diagonal + down
                    if layer < layers - 1:
                        down = 0.5 * harmonic(here[layer], here[layer + 1])
                        face_z[layer, x - 1] = down
                        diagonal = diagonal + down
                    if layer == 0:
                        diagonal = diagonal + col_cond[pl.ds(x - 1, 1), :]
                    inverse[layer, x - 1] = 1.0 / diagonal
                here, before = after, ahead
            return here, before

        return lax.fori_loop(0, (stop - start) // size, step, carry)

    def relax(head, x, which, with_river):
        now = {layer: head[layer, x] for layer in range(layers)
               if any(abs(layer - other) < 2 for other in which)}
        results = []
        for layer in which:
            along = face_y[layer, x - 1]
            total = source[x - 1] if layer == 0 and with_river else base[layer, x - 1]
            total = total + face_x[layer, x] * head[layer, x + 1]
            total = total + face_x[layer, x - 1] * head[layer, x - 1]
            total = total + along * pltpu.roll(now[layer], width - 1, 1)
            total = total + pltpu.roll(along * now[layer], 1, 1)
            if layer < layers - 1:
                total = total + face_z[layer, x - 1] * now[layer + 1]
            if layer > 0:
                total = total + face_z[layer - 1, x - 1] * now[layer - 1]
            results.append(total * inverse[layer, x - 1])
        return results

    every = list(range(layers))
    lower = every[1:]

    def sweep(index, which, with_river=True):
        def body(block):
            results = [relax(heads[index], x, which, with_river) for x in block]
            for x, result in zip(block, results):
                for layer, value in zip(which, result):
                    heads[index + 1][layer, x] = value
        return body

    def sweep_and_send(index):
        body = sweep(index, every)
        body([1])
        body([rows])
        copies = halo(index + 1)
        over(2, rows, 3, body)
        return copies

    def received(copies):
        for copy in copies:
            copy.wait_recv()

    def by_group(values):
        return jnp.concatenate([values[:, g * LANES:(g + 1) * LANES] for g in range(groups)], axis=0)

    def with_rate(rates, values):
        return jnp.concatenate(
            [rates[g:g + 1, :] * values[:, g * LANES:(g + 1) * LANES] for g in range(groups)], axis=1)

    def fetch(bucket, sections):
        left = jnp.concatenate(halves(by_group(sections)), axis=1)
        wide = slot_range(bucket)
        picked = jnp.dot(left, one_r[:, wide], preferred_element_type=F32)
        value = jnp.zeros((members, slots), F32)
        high = reach_high[own(bucket), :]
        for g in range(groups):
            value = value + jnp.where(high == g, picked[g * members:(g + 1) * members], 0.0)
        fetched[bucket] = value
        flow = weight[own(bucket), :] * value
        for part, term in enumerate(halves(jnp.concatenate([flow, flow], axis=0))):
            spread[part * rows * members:(part + 1) * rows * members, wide] = (
                mask_x[:, wide] * jnp.concatenate([term] * (rows // 2), axis=0))

    def river_sum(first, last):
        wide = slice(first * slots, last * slots)
        sums = dot_rows(spread[:, wide], one_y[:width, wide])
        return (sums[:rows * members] + sums[rows * members:]).reshape(rows, members, width)

    def top_terms(head):
        return jnp.concatenate(halves(head[0, 1:rows + 1].reshape(rows * members, width)), axis=1)

    def leak_part(terms, bucket, parts):
        wide = slot_range(bucket)
        picked = jnp.dot(terms, one_y[:, wide], preferred_element_type=F32)
        value = jnp.zeros((members, slots), F32)
        position = column_x[own(bucket), :]
        for x in range(rows):
            value = value + jnp.where(position == x, picked[x * members:(x + 1) * members], 0.0)
        flow = weight[own(bucket), :] * (fetched[bucket] - value)
        high = reach_high[own(bucket), :]
        split = jnp.concatenate([jnp.where(high == g, flow, 0.0) for g in range(groups)], axis=0)
        sums = dot_rows(jnp.concatenate(halves(split), axis=0), one_r[:LANES, wide])
        sums = sums[:groups * members] + sums[groups * members:]
        for g in range(groups):
            parts[bucket, :, g * LANES:(g + 1) * LANES] = sums[g * members:(g + 1) * members]

    def send_part(step, bucket, parts, got):
        return send(parts.at[bucket], got.at[bucket], leak_send.at[step, bucket],
                    leak_recv.at[step, bucket], owner(bucket))

    def near_leak(parts, got):
        values = parts[NEAR]
        for bucket in near:
            values = values + got[bucket]
        return values

    received(halos)
    link(head0, 1, rows + 1, link_start(head0))
    for bucket in [NEAR] + near:
        if bucket != NEAR:
            first_sections[bucket].wait_recv()
        fetch(bucket, section[...] if bucket == NEAR else sect0[bucket])
    first_sections[FAR].wait_recv()
    fetch(FAR, sect0[FAR])
    source[...] = base[0] + river_sum(0, buckets)
    halos = sweep_and_send(0)
    received(halos)
    halos = sweep_and_send(1)
    received(halos)

    over(1, rows + 1, 4, sweep(2, every[:1]))
    terms = top_terms(head3)
    leak_part(terms, FAR, part1)
    copies = {FAR: send_part(0, FAR, part1, got1)}
    sweep(2, lower)([1])
    sweep(2, lower)([rows])
    halos = halo(3)
    for bucket in near:
        leak_part(terms, bucket, part1)
        copies[bucket] = send_part(0, bucket, part1, got1)
    leak_part(terms, NEAR, part1)
    over(2, rows, 3, sweep(2, lower))
    received(halos)
    half = rows // 2 + 1
    carry = link(head3, 1, half, link_start(head3))

    loads["inflow"].wait()
    rate_copy.wait_recv()
    for bucket in near:
        copies[bucket].wait_recv()
    partial_state[...] = section[...] + with_rate(rate, inflow[...] - near_leak(part1, got1))
    state_copy = send(partial_state, state_got, state_send, state_recv, user(FAR))
    link(head3, half, rows + 1, carry)
    copies[FAR].wait_recv()
    sect1[NEAR] = partial_state[...] - with_rate(rate, got1[FAR])
    second_sections = {
        bucket: send(sect1.at[NEAR], sect1.at[bucket], sect_send.at[1, bucket], sect_recv.at[1, bucket], user(bucket))
        for bucket in near}

    over(1, rows + 1, 4, sweep(3, every, False))
    for bucket in [NEAR] + near:
        if bucket != NEAR:
            second_sections[bucket].wait_recv()
        fetch(bucket, sect1[bucket])
    river[...] = river_sum(0, FAR)
    state_copy.wait_recv()
    fetch(FAR, state_got[...] - with_rate(rate_got, part1[FAR]))
    river[...] = river[...] + river_sum(FAR, buckets)
    source[...] = base[0] + river[...]

    def add_river(block):
        for x in block:
            head4[0, x] = head4[0, x] + river[x - 1] * inverse[0, x - 1]

    add_river([1, rows])
    halos = halo(4)
    over(2, rows, 6, add_river)
    received(halos)
    halos = sweep_and_send(4)
    received(halos)
    over(1, rows + 1, 4, sweep(5, every[:1]))
    terms = top_terms(head6)
    leak_part(terms, FAR, part2)
    copies = {FAR: send_part(1, FAR, part2, got2)}
    for bucket in near:
        leak_part(terms, bucket, part2)
        copies[bucket] = send_part(1, bucket, part2, got2)
    leak_part(terms, NEAR, part2)
    over(1, rows + 1, 4, sweep(5, lower))
    stores = [pltpu.make_async_copy(head6.at[:, 1:rows + 1, m, :], head_out.at[m], store_sem.at[m])
              for m in range(members)]
    for copy in stores:
        copy.start()
    for bucket in near:
        copies[bucket].wait_recv()
    values = near_leak(part2, got2)
    copies[FAR].wait_recv()
    section_out[...] = section[...] + with_rate(rate, inflow[...] - (values + got2[FAR]))
    for copy in stores:
        copy.wait()
    for copy in sends:
        copy.wait_send()


def body(tile_count, head_start, recharge, section_start, inflow, soil_class, class_conduct, class_alpha,
         capacity, river_cell, river_reach, river_cond, reach_rate):
    members, layers, rows, width = head_start.shape
    buckets, slots = river_cell.shape[1:]
    lines = buckets * slots // LANES
    reaches = section_start.shape[1]
    groups = reaches // LANES
    any_spec = pl.BlockSpec(memory_space=pl.ANY)
    smem_spec = pl.BlockSpec(memory_space=pltpu.SMEM)
    vmem_spec = pl.BlockSpec(memory_space=pltpu.VMEM)
    vmem = pltpu.VMEM
    dma = pltpu.SemaphoreType.DMA
    grid = (layers, rows, members, width)
    state = (members, reaches)
    every = buckets * slots
    scratch = [vmem((layers, rows + 2, members, width), F32)] * (PICARD * SWEEPS + 1) + [
        vmem((rows, members, width), F32),
        vmem(state, F32), vmem(state, F32), vmem((layers, rows, width), jnp.int32), vmem((layers, rows, width), F32),
        vmem((lines, LANES), jnp.int32), vmem((lines, LANES), jnp.int32), vmem((lines, LANES), F32),
        vmem((groups, LANES), F32),
        vmem((layers, rows + 8, width), F32), vmem((layers, rows + 8, width), F32),
        vmem(grid, F32), vmem((rows, members, width), F32),
        vmem((layers, rows + 1, members, width), F32), vmem(grid, F32),
        vmem((layers - 1, rows, members, width), F32), vmem(grid, F32), vmem((rows, width), F32),
        vmem((2 * width, every), BF16), vmem((rows * members, every), BF16), vmem((2 * LANES, every), BF16),
        vmem((2 * rows * members, every), BF16),
    ] + [vmem((buckets, slots), F32)] * 5 + [
        vmem((buckets, members, slots), F32), vmem((rows, members, width), F32),
        vmem((2, 2 * layers, width), F32), vmem((2, 2 * layers, width), F32),
    ] + [vmem((buckets,) + state, F32)] * 6 + [vmem(state, F32)] * 2 + [vmem((groups, LANES), F32)] + [
        dma((8,)), dma((members,)), dma((members,)), dma((members,)),
        dma((PICARD * SWEEPS, 2)), dma((PICARD * SWEEPS, 2)), dma((2,)), dma((2,)),
        dma((2, buckets)), dma((2, buckets)), dma((2, buckets)), dma((2, buckets)),
        dma, dma, dma, dma,
    ]
    return pl.pallas_call(
        functools.partial(kernel, tile_count),
        out_shape=(vmem(head_start.shape, F32), vmem(state, F32)),
        in_specs=[any_spec] * 5 + [smem_spec] * 2 + [any_spec] * 5,
        out_specs=(vmem_spec, vmem_spec),
        scratch_shapes=scratch,
        compiler_params=pltpu.CompilerParams(
            collective_id=0, has_side_effects=True, vmem_limit_bytes=52 * 1024 * 1024),
        name="aquifer",
    )(head_start, recharge, section_start, inflow, soil_class, class_conduct, class_alpha, capacity,
      river_cell.reshape(lines, LANES), river_reach.reshape(lines, LANES), river_cond.reshape(lines, LANES),
      reach_rate.reshape(groups, LANES))


def solution(mesh):
    return jax.shard_map(
        functools.partial(body, mesh.shape["space"]),
        mesh=mesh,
        in_specs=(
            P("member", None, "space", None),
            P("member", "space", None),
            P("member", "space"),
            P("member", "space"),
            P(None, "space", None),
            P(),
            P(),
            P(None, "space", None),
            P("space", None, None),
            P("space", None, None),
            P("space", None, None),
            P("space"),
        ),
        out_specs=(P("member", None, "space", None), P("member", "space")),
        check_vma=False,
    )
```

```python
import functools

import jax
import jax.numpy as jnp
from jax import lax
from jax.experimental import pallas as pl
from jax.experimental.pallas import tpu as pltpu
from jax.sharding import PartitionSpec as P

PICARD = 2
SWEEPS = 3
NEAR = 2
FAR = 2 * NEAR + 1
LANES = 128
F32 = jnp.float32
BF16 = jnp.bfloat16


def halves(values):
    high = values.astype(BF16)
    return high, (values - high.astype(F32)).astype(BF16)


def dot_rows(left, right):
    return lax.dot_general(left, right, (((1,), (1,)), ((), ())), preferred_element_type=F32)


def kernel(
    tile_count,
    head_in, recharge_in, section_in, inflow_in, soil_in, class_conduct, class_alpha,
    capacity_in, cell_in, reach_in, cond_in, rate_in,
    head_out, section_out,
    head0, head1, head2, head3, head4, head5, head6,
    recharge, section, inflow, soil, capacity, cell, reach, cond, rate,
    kc, ka, base, source, face_x, face_y, face_z, inverse, col_cond,
    one_y, mask_x, one_r, spread, weight, column_x, column_y, reach_high, reach_low, fetched, river,
    edge, edge_got, sect0, sect1, part1, part2, got1, got2, partial_state, state_got, rate_got,
    load_sem, head_sem, recharge_sem, store_sem, halo_send, halo_recv, edge_send, edge_recv,
    sect_send, sect_recv, leak_send, leak_recv, state_send, state_recv, rate_send, rate_recv,
):
    me = lax.axis_index("space")
    heads = (head0, head1, head2, head3, head4, head5, head6)
    layers, padded, members, width = head0.shape
    rows = padded - 2
    buckets, slots = weight.shape
    pieces = slots // LANES
    groups = section.shape[1] // LANES
    near = [bucket for bucket in range(buckets) if bucket not in (NEAR, FAR)]
    remote = near + [FAR]

    def tile(shift):
        return lax.rem(me + shift + tile_count, tile_count)

    def user(bucket):
        return tile(tile_count // 2 if bucket == FAR else NEAR - bucket)

    def owner(bucket):
        return tile(tile_count // 2 if bucket == FAR else bucket - NEAR)

    def own(bucket):
        return slice(bucket, bucket + 1)

    def slot_range(bucket):
        return slice(bucket * slots, (bucket + 1) * slots)

    sends = []

    def send(source_ref, target_ref, send_sem, recv_sem, device):
        copy = pltpu.make_async_remote_copy(
            src_ref=source_ref, dst_ref=target_ref, send_sem=send_sem, recv_sem=recv_sem,
            device_id={"space": device}, device_id_type=pl.DeviceIdType.MESH)
        copy.start()
        sends.append(copy)
        return copy

    def over(start, stop, size, body):
        def step(count, carry):
            body([start + count * size + offset for offset in range(size)])
            return carry
        lax.fori_loop(0, (stop - start) // size, step, 0)

    loads = {}
    pairs = [("soil", soil_in, soil), ("section", section_in, section), ("rate", rate_in, rate),
             ("cell", cell_in, cell), ("reach", reach_in, reach), ("cond", cond_in, cond)]
    for index, (name, source_ref, target_ref) in enumerate(pairs):
        loads[name] = pltpu.make_async_copy(source_ref, target_ref, load_sem.at[index])
        loads[name].start()
    head_loads = [pltpu.make_async_copy(head_in.at[m], head0.at[:, 1:rows + 1, m, :], head_sem.at[m])
                  for m in range(members)]
    for copy in head_loads:
        copy.start()
    for index, (name, source_ref, target_ref) in enumerate(
            [("capacity", capacity_in, capacity), ("inflow", inflow_in, inflow)]):
        loads[name] = pltpu.make_async_copy(source_ref, target_ref, load_sem.at[len(pairs) + index])
        loads[name].start()
    recharge_loads = [pltpu.make_async_copy(recharge_in.at[m], recharge.at[:, m, :], recharge_sem.at[m])
                      for m in range(members)]
    for copy in recharge_loads:
        copy.start()

    barrier = pltpu.get_barrier_semaphore()
    for bucket in remote:
        pl.semaphore_signal(barrier, inc=1, device_id={"space": user(bucket)},
                            device_id_type=pl.DeviceIdType.MESH)

    loads["soil"].wait()
    classes = soil[...]
    conduct_of = jnp.zeros(classes.shape, F32)
    alpha_of = jnp.zeros(classes.shape, F32)
    for index in range(class_conduct.shape[0]):
        match = classes == index
        conduct_of = jnp.where(match, 2.0 * class_conduct[index], conduct_of)
        alpha_of = jnp.where(match, class_alpha[index], alpha_of)
    kc[:, 1:rows + 1, :] = conduct_of
    ka[:, 1:rows + 1, :] = alpha_of
    for side, row in ((0, 0), (1, rows - 1)):
        for layer in range(layers):
            edge[side, layer:layer + 1, :] = conduct_of[layer, row:row + 1, :]
            edge[side, layers + layer:layers + layer + 1, :] = alpha_of[layer, row:row + 1, :]

    loads["cell"].wait()
    loads["reach"].wait()
    loads["cond"].wait()
    live = reach[...] >= 0
    columns = jnp.where(live, cell[...], 0)
    reaches = jnp.where(live, reach[...], 0)
    for target_ref, values in (
            (weight, jnp.where(live, cond[...], 0.0)),
            (column_x, columns // width), (column_y, columns % width),
            (reach_high, reaches // LANES), (reach_low, reaches % LANES)):
        for bucket in range(buckets):
            for piece in range(pieces):
                line = bucket * pieces + piece
                target_ref[own(bucket), piece * LANES:(piece + 1) * LANES] = (
                    values[line:line + 1, :].astype(F32))

    def one_hot(ids, row):
        rows16 = jnp.broadcast_to(row, (16, slots)).astype(BF16)
        wide = jnp.concatenate([rows16] * (ids.shape[0] // 16), axis=0)
        return jnp.where(ids == wide, jnp.ones((), BF16), jnp.zeros((), BF16))

    ids = lax.broadcasted_iota(jnp.int32, (width, slots), 0)
    y_ids = ids.astype(F32).astype(BF16)
    x_ids = (ids // members).astype(F32).astype(BF16)
    r_ids = (ids % LANES).astype(F32).astype(BF16)

    def build(bucket):
        wide = slot_range(bucket)
        values = one_hot(y_ids, column_y[own(bucket), :])
        one_y[:width, wide] = values
        one_y[width:, wide] = values
        mask_x[:, wide] = one_hot(x_ids, column_x[own(bucket), :])
        one_r[:, wide] = one_hot(r_ids, reach_low[own(bucket), :])

    build(0)
    build(1)
    build(2)

    pl.semaphore_wait(barrier, len(remote))

    loads["section"].wait()
    loads["rate"].wait()
    first_sections = {}
    for bucket in [FAR] + near:
        first_sections[bucket] = send(
            section, sect0.at[bucket], sect_send.at[0, bucket], sect_recv.at[0, bucket], user(bucket))
    rate_copy = send(rate, rate_got, rate_send, rate_recv, user(FAR))
    edge_copies = [
        send(edge.at[side], edge_got.at[1 - side], edge_send.at[side], edge_recv.at[1 - side], tile(shift))
        for side, shift in ((0, -1), (1, 1))]

    def halo(index):
        return [
            send(heads[index].at[:, 1], heads[index].at[:, rows + 1],
                 halo_send.at[index, 0], halo_recv.at[index, 1], tile(-1)),
            send(heads[index].at[:, rows], heads[index].at[:, 0],
                 halo_send.at[index, 1], halo_recv.at[index, 0], tile(1)),
        ]

    for copy in head_loads:
        copy.wait()
    halos = halo(0)

    for bucket in range(3, buckets):
        build(bucket)
    flat = lax.broadcasted_iota(jnp.int32, (rows, slots), 0).astype(F32)
    total = jnp.zeros((2 * rows, width), F32)
    for bucket in range(buckets):
        terms = jnp.where(flat == column_x[own(bucket), :], weight[own(bucket), :], 0.0)
        total = total + dot_rows(jnp.concatenate(halves(terms), axis=0), one_y[:width, slot_range(bucket)])
    col_cond[...] = total[:rows] + total[rows:]

    loads["capacity"].wait()
    for copy in recharge_loads:
        copy.wait()

    def begin(block):
        for x in block:
            for layer in range(layers):
                term = capacity[layer, pl.ds(x, 1), :] * head0[layer, x + 1]
                base[layer, x] = term + recharge[x] if layer == 0 else term

    over(0, rows, 2, begin)

    for copy in edge_copies:
        copy.wait_recv()
    for side, row, outside in ((0, 0, 0), (1, rows + 1, tile_count - 1)):
        inside = jnp.where(me == outside, 0.0, 1.0)
        for layer in range(layers):
            kc[layer, row:row + 1, :] = edge_got[side, layer:layer + 1, :] * inside
            ka[layer, row:row + 1, :] = edge_got[side, layers + layer:layers + layer + 1, :]

    lane = lax.broadcasted_iota(jnp.int32, (members, width), 1)

    def harmonic(first, second):
        return first * second / (first + second)

    def conduct(head, x):
        return tuple(
            kc[layer, pl.ds(x, 1), :]
            * jnp.exp(ka[layer, pl.ds(x, 1), :] * jnp.minimum(head[layer, x], 0.0))
            for layer in range(layers))

    def link_start(head):
        low = conduct(head, 0)
        here = conduct(head, 1)
        before = tuple(harmonic(a, b) for a, b in zip(low, here))
        for layer in range(layers):
            face_x[layer, 0] = before[layer]
        return here, before

    def link(head, start, stop, carry):
        size = 2

        def step(count, carry):
            here, before = carry
            for offset in range(size):
                x = start + count * size + offset
                after = conduct(head, x + 1)
                ahead = tuple(harmonic(a, b) for a, b in zip(here, after))
                down = None
                for layer in range(layers):
                    face_x[layer, x] = ahead[layer]
                    along = harmonic(here[layer], pltpu.roll(here[layer], width - 1, 1))
                    along = jnp.where(lane == width - 1, 0.0, along)
                    face_y[layer, x - 1] = along
                    diagonal = capacity[layer, pl.ds(x - 1, 1), :] + ahead[layer] + before[layer]
                    diagonal = diagonal + along + pltpu.roll(along, 1, 1)
                    if layer > 0:
                        diagonal = diagonal + down
                    if layer < layers - 1:
                        down = 0.5 * harmonic(here[layer], here[layer + 1])
                        face_z[layer, x - 1] = down
                        diagonal = diagonal + down
                    if layer == 0:
                        diagonal = diagonal + col_cond[pl.ds(x - 1, 1), :]
                    inverse[layer, x - 1] = 1.0 / diagonal
                here, before = after, ahead
            return here, before

        return lax.fori_loop(0, (stop - start) // size, step, carry)

    def relax(head, x, which, with_river):
        now = {layer: head[layer, x] for layer in range(layers)
               if any(abs(layer - other) < 2 for other in which)}
        results = []
        for layer in which:
            along = face_y[layer, x - 1]
            total = source[x - 1] if layer == 0 and with_river else base[layer, x - 1]
            total = total + face_x[layer, x] * head[layer, x + 1]
            total = total + face_x[layer, x - 1] * head[layer, x - 1]
            total = total + along * pltpu.roll(now[layer], width - 1, 1)
            total = total + pltpu.roll(along * now[layer], 1, 1)
            if layer < layers - 1:
                total = total + face_z[layer, x - 1] * now[layer + 1]
            if layer > 0:
                total = total + face_z[layer - 1, x - 1] * now[layer - 1]
            results.append(total * inverse[layer, x - 1])
        return results

    every = list(range(layers))
    lower = every[1:]

    def sweep(index, which, with_river=True):
        def body(block):
            results = [relax(heads[index], x, which, with_river) for x in block]
            for x, result in zip(block, results):
                for layer, value in zip(which, result):
                    heads[index + 1][layer, x] = value
        return body

    def sweep_and_send(index):
        body = sweep(index, every)
        body([1])
        body([rows])
        copies = halo(index + 1)
        over(2, rows, 3, body)
        return copies

    def received(copies):
        for copy in copies:
            copy.wait_recv()

    def by_group(values):
        return jnp.concatenate([values[:, g * LANES:(g + 1) * LANES] for g in range(groups)], axis=0)

    def with_rate(rates, values):
        return jnp.concatenate(
            [rates[g:g + 1, :] * values[:, g * LANES:(g + 1) * LANES] for g in range(groups)], axis=1)

    def fetch(bucket, sections):
        left = jnp.concatenate(halves(by_group(sections)), axis=1)
        wide = slot_range(bucket)
        picked = jnp.dot(left, one_r[:, wide], preferred_element_type=F32)
        value = jnp.zeros((members, slots), F32)
        high = reach_high[own(bucket), :]
        for g in range(groups):
            value = value + jnp.where(high == g, picked[g * members:(g + 1) * members], 0.0)
        fetched[bucket] = value
        flow = weight[own(bucket), :] * value
        for part, term in enumerate(halves(jnp.concatenate([flow, flow], axis=0))):
            spread[part * rows * members:(part + 1) * rows * members, wide] = (
                mask_x[:, wide] * jnp.concatenate([term] * (rows // 2), axis=0))

    def river_sum(first, last):
        wide = slice(first * slots, last * slots)
        sums = dot_rows(spread[:, wide], one_y[:width, wide])
        return (sums[:rows * members] + sums[rows * members:]).reshape(rows, members, width)

    def top_terms(head):
        return jnp.concatenate(halves(head[0, 1:rows + 1].reshape(rows * members, width)), axis=1)

    def leak_part(terms, bucket, parts):
        wide = slot_range(bucket)
        picked = jnp.dot(terms, one_y[:, wide], preferred_element_type=F32)
        value = jnp.zeros((members, slots), F32)
        position = column_x[own(bucket), :]
        for x in range(rows):
            value = value + jnp.where(position == x, picked[x * members:(x + 1) * members], 0.0)
        flow = weight[own(bucket), :] * (fetched[bucket] - value)
        high = reach_high[own(bucket), :]
        split = jnp.concatenate([jnp.where(high == g, flow, 0.0) for g in range(groups)], axis=0)
        sums = dot_rows(jnp.concatenate(halves(split), axis=0), one_r[:LANES, wide])
        sums = sums[:groups * members] + sums[groups * members:]
        for g in range(groups):
            parts[bucket, :, g * LANES:(g + 1) * LANES] = sums[g * members:(g + 1) * members]

    def send_part(step, bucket, parts, got):
        return send(parts.at[bucket], got.at[bucket], leak_send.at[step, bucket],
                    leak_recv.at[step, bucket], owner(bucket))

    def near_leak(parts, got):
        values = parts[NEAR]
        for bucket in near:
            values = values + got[bucket]
        return values

    received(halos)
    link(head0, 1, rows + 1, link_start(head0))
    for bucket in [NEAR] + near:
        if bucket != NEAR:
            first_sections[bucket].wait_recv()
        fetch(bucket, section[...] if bucket == NEAR else sect0[bucket])
    first_sections[FAR].wait_recv()
    fetch(FAR, sect0[FAR])
    source[...] = base[0] + river_sum(0, buckets)
    halos = sweep_and_send(0)
    received(halos)
    halos = sweep_and_send(1)
    received(halos)

    over(1, rows + 1, 4, sweep(2, every[:1]))
    terms = top_terms(head3)
    leak_part(terms, FAR, part1)
    copies = {FAR: send_part(0, FAR, part1, got1)}
    sweep(2, lower)([1])
    sweep(2, lower)([rows])
    halos = halo(3)
    for bucket in near:
        leak_part(terms, bucket, part1)
        copies[bucket] = send_part(0, bucket, part1, got1)
    leak_part(terms, NEAR, part1)
    over(2, rows, 3, sweep(2, lower))
    received(halos)
    half = rows // 2 + 1
    carry = link(head3, 1, half, link_start(head3))

    loads["inflow"].wait()
    rate_copy.wait_recv()
    for bucket in near:
        copies[bucket].wait_recv()
    partial_state[...] = section[...] + with_rate(rate, inflow[...] - near_leak(part1, got1))
    state_copy = send(partial_state, state_got, state_send, state_recv, user(FAR))
    link(head3, half, rows + 1, carry)
    copies[FAR].wait_recv()
    sect1[NEAR] = partial_state[...] - with_rate(rate, got1[FAR])
    second_sections = {
        bucket: send(sect1.at[NEAR], sect1.at[bucket], sect_send.at[1, bucket], sect_recv.at[1, bucket], user(bucket))
        for bucket in near}

    over(1, rows + 1, 4, sweep(3, every, False))
    for bucket in [NEAR] + near:
        if bucket != NEAR:
            second_sections[bucket].wait_recv()
        fetch(bucket, sect1[bucket])
    river[...] = river_sum(0, FAR)
    state_copy.wait_recv()
    fetch(FAR, state_got[...] - with_rate(rate_got, part1[FAR]))
    river[...] = river[...] + river_sum(FAR, buckets)
    source[...] = base[0] + river[...]

    def add_river(block):
        for x in block:
            head4[0, x] = head4[0, x] + river[x - 1] * inverse[0, x - 1]

    add_river([1, rows])
    halos = halo(4)
    over(2, rows, 6, add_river)
    received(halos)
    halos = sweep_and_send(4)
    received(halos)
    over(1, rows + 1, 4, sweep(5, every[:1]))
    terms = top_terms(head6)
    leak_part(terms, FAR, part2)
    copies = {FAR: send_part(1, FAR, part2, got2)}
    for bucket in near:
        leak_part(terms, bucket, part2)
        copies[bucket] = send_part(1, bucket, part2, got2)
    leak_part(terms, NEAR, part2)
    over(1, rows + 1, 4, sweep(5, lower))
    stores = [pltpu.make_async_copy(head6.at[:, 1:rows + 1, m, :], head_out.at[m], store_sem.at[m])
              for m in range(members)]
    for copy in stores:
        copy.start()
    for bucket in near:
        copies[bucket].wait_recv()
    values = near_leak(part2, got2)
    copies[FAR].wait_recv()
    section_out[...] = section[...] + with_rate(rate, inflow[...] - (values + got2[FAR]))
    for copy in stores:
        copy.wait()
    for copy in sends:
        copy.wait_send()


def body(tile_count, head_start, recharge, section_start, inflow, soil_class, class_conduct, class_alpha,
         capacity, river_cell, river_reach, river_cond, reach_rate):
    members, layers, rows, width = head_start.shape
    buckets, slots = river_cell.shape[1:]
    lines = buckets * slots // LANES
    reaches = section_start.shape[1]
    groups = reaches // LANES
    any_spec = pl.BlockSpec(memory_space=pltpu.HBM)
    smem_spec = pl.BlockSpec(memory_space=pltpu.SMEM)
    vmem_spec = pl.BlockSpec(memory_space=pltpu.VMEM)
    vmem = pltpu.VMEM
    dma = pltpu.SemaphoreType.DMA
    grid = (layers, rows, members, width)
    state = (members, reaches)
    every = buckets * slots
    scratch = [vmem((layers, rows + 2, members, width), F32)] * (PICARD * SWEEPS + 1) + [
        vmem((rows, members, width), F32),
        vmem(state, F32), vmem(state, F32), vmem((layers, rows, width), jnp.int32), vmem((layers, rows, width), F32),
        vmem((lines, LANES), jnp.int32), vmem((lines, LANES), jnp.int32), vmem((lines, LANES), F32),
        vmem((groups, LANES), F32),
        vmem((layers, rows + 8, width), F32), vmem((layers, rows + 8, width), F32),
        vmem(grid, F32), vmem((rows, members, width), F32),
        vmem((layers, rows + 1, members, width), F32), vmem(grid, F32),
        vmem((layers - 1, rows, members, width), F32), vmem(grid, F32), vmem((rows, width), F32),
        vmem((2 * width, every), BF16), vmem((rows * members, every), BF16), vmem((2 * LANES, every), BF16),
        vmem((2 * rows * members, every), BF16),
    ] + [vmem((buckets, slots), F32)] * 5 + [
        vmem((buckets, members, slots), F32), vmem((rows, members, width), F32),
        vmem((2, 2 * layers, width), F32), vmem((2, 2 * layers, width), F32),
    ] + [vmem((buckets,) + state, F32)] * 6 + [vmem(state, F32)] * 2 + [vmem((groups, LANES), F32)] + [
        dma((8,)), dma((members,)), dma((members,)), dma((members,)),
        dma((PICARD * SWEEPS, 2)), dma((PICARD * SWEEPS, 2)), dma((2,)), dma((2,)),
        dma((2, buckets)), dma((2, buckets)), dma((2, buckets)), dma((2, buckets)),
        dma, dma, dma, dma,
    ]
    return pl.pallas_call(
        functools.partial(kernel, tile_count),
        out_shape=(vmem(head_start.shape, F32), vmem(state, F32)),
        in_specs=[any_spec] * 5 + [smem_spec] * 2 + [any_spec] * 5,
        out_specs=(vmem_spec, vmem_spec),
        scratch_shapes=scratch,
        compiler_params=pltpu.CompilerParams(
            collective_id=0, has_side_effects=True, vmem_limit_bytes=62 * 1024 * 1024),
        name="aquifer",
    )(head_start, recharge, section_start, inflow, soil_class, class_conduct, class_alpha, capacity,
      river_cell.reshape(lines, LANES), river_reach.reshape(lines, LANES), river_cond.reshape(lines, LANES),
      reach_rate.reshape(groups, LANES))


def solution(mesh):
    return jax.shard_map(
        functools.partial(body, mesh.shape["space"]),
        mesh=mesh,
        in_specs=(
            P("member", None, "space", None),
            P("member", "space", None),
            P("member", "space"),
            P("member", "space"),
            P(None, "space", None),
            P(),
            P(),
            P(None, "space", None),
            P("space", None, None),
            P("space", None, None),
            P("space", None, None),
            P("space"),
        ),
        out_specs=(P("member", None, "space", None), P("member", "space")),
        check_vma=False,
    )
```

```python
import functools

import jax
import jax.numpy as jnp
from jax import lax
from jax.experimental import pallas as pl
from jax.experimental.pallas import tpu as pltpu
from jax.sharding import PartitionSpec as P

PICARD = 2
SWEEPS = 3
NEAR = 2
FAR = 2 * NEAR + 1
LANES = 128
F32 = jnp.float32
BF16 = jnp.bfloat16


def halves(values):
    high = values.astype(BF16)
    return high, (values - high.astype(F32)).astype(BF16)


def dot_rows(left, right):
    return lax.dot_general(left, right, (((1,), (1,)), ((), ())), preferred_element_type=F32)


def kernel(
    tile_count,
    head_in, recharge_in, section_in, inflow_in, soil_in, class_conduct, class_alpha,
    capacity_in, cell_in, reach_in, cond_in, rate_in,
    head_out, section_out,
    head0, head1, head2, head3, head4, head5, head6,
    recharge, section, inflow, soil, capacity_own, cell, reach, cond, rate,
    kc, ka, capacity, base, source, face_x, face_y, face_z, inverse, col_cond, river0, river1,
    one_y, mask_x, one_r, spread, weight, column_x, column_y, reach_high, reach_low, fetched,
    edge, edge_got, col_edge, col_got,
    sect0, sect1, part1, part2, got1, got2, partial_state, state_got, rate_got,
    load_sem, head_sem, recharge_sem, store_sem, halo_send, halo_recv, edge_send, edge_recv,
    rain_send, rain_recv, col_send, col_recv, river_send, river_recv,
    sect_send, sect_recv, leak_send, leak_recv, state_send, state_recv, rate_send, rate_recv,
):
    me = lax.axis_index("space")
    heads = (head0, head1, head2, head3, head4, head5, head6)
    layers, padded, members, width = head0.shape
    deep = SWEEPS
    rows = padded - 2 * deep
    first, last = deep, deep + rows - 1
    buckets, slots = weight.shape
    pieces = slots // LANES
    groups = section.shape[1] // LANES
    near = [bucket for bucket in range(buckets) if bucket not in (NEAR, FAR)]
    remote = near + [FAR]

    def tile(shift):
        return lax.rem(me + shift + tile_count, tile_count)

    def user(bucket):
        return tile(tile_count // 2 if bucket == FAR else NEAR - bucket)

    def owner(bucket):
        return tile(tile_count // 2 if bucket == FAR else bucket - NEAR)

    def own(bucket):
        return slice(bucket, bucket + 1)

    def slot_range(bucket):
        return slice(bucket * slots, (bucket + 1) * slots)

    sends = []

    def send(source_ref, target_ref, send_sem, recv_sem, device):
        copy = pltpu.make_async_remote_copy(
            src_ref=source_ref, dst_ref=target_ref, send_sem=send_sem, recv_sem=recv_sem,
            device_id={"space": device}, device_id_type=pl.DeviceIdType.MESH)
        copy.start()
        sends.append(copy)
        return copy

    def over(start, stop, size, body):
        def step(count, carry):
            body([start + count * size + offset for offset in range(size)])
            return carry
        lax.fori_loop(0, (stop - start) // size, step, 0)

    loads = {}
    pairs = [("soil", soil_in, soil), ("capacity", capacity_in, capacity_own), ("section", section_in, section), ("rate", rate_in, rate),
             ("cell", cell_in, cell), ("reach", reach_in, reach), ("cond", cond_in, cond)]
    for index, (name, source_ref, target_ref) in enumerate(pairs):
        loads[name] = pltpu.make_async_copy(source_ref, target_ref, load_sem.at[index])
        loads[name].start()
    head_loads = [pltpu.make_async_copy(head_in.at[m], head0.at[:, first:last + 1, m, :], head_sem.at[m])
                  for m in range(members)]
    for copy in head_loads:
        copy.start()
    for index, (name, source_ref, target_ref) in enumerate(
            [("inflow", inflow_in, inflow)]):
        loads[name] = pltpu.make_async_copy(source_ref, target_ref, load_sem.at[len(pairs) + index])
        loads[name].start()
    recharge_loads = [pltpu.make_async_copy(recharge_in.at[m], recharge.at[first:last + 1, m, :], recharge_sem.at[m])
                      for m in range(members)]
    for copy in recharge_loads:
        copy.start()

    barrier = pltpu.get_barrier_semaphore()
    for bucket in remote:
        pl.semaphore_signal(barrier, inc=1, device_id={"space": user(bucket)},
                            device_id_type=pl.DeviceIdType.MESH)

    loads["soil"].wait()
    classes = soil[...]
    conduct_of = jnp.zeros(classes.shape, F32)
    alpha_of = jnp.zeros(classes.shape, F32)
    for index in range(class_conduct.shape[0]):
        match = classes == index
        conduct_of = jnp.where(match, 2.0 * class_conduct[index], conduct_of)
        alpha_of = jnp.where(match, class_alpha[index], alpha_of)
    kc[:, first:last + 1, :] = conduct_of
    ka[:, first:last + 1, :] = alpha_of
    loads["capacity"].wait()
    capacity_of = capacity_own[...]
    capacity[:, first:last + 1, :] = capacity_of
    packed = [(kc, conduct_of, deep), (ka, alpha_of, deep), (capacity, capacity_of, deep - 1)]
    for side in range(2):
        line = 0
        for _, values, depth in packed:
            for layer in range(layers):
                start = 0 if side == 0 else rows - depth
                edge[side, line:line + depth, :] = values[layer, start:start + depth, :]
                line += depth

    pl.semaphore_wait(barrier, len(remote))

    loads["section"].wait()
    loads["rate"].wait()
    first_sections = {}
    for bucket in [FAR] + near:
        first_sections[bucket] = send(
            section, sect0.at[bucket], sect_send.at[0, bucket], sect_recv.at[0, bucket], user(bucket))
    rate_copy = send(rate, rate_got, rate_send, rate_recv, user(FAR))
    beside = [
        send(edge.at[side], edge_got.at[1 - side], edge_send.at[side], edge_recv.at[1 - side], tile(shift))
        for side, shift in ((0, -1), (1, 1))]

    def halo(index):
        step = index // SWEEPS
        return [
            send(heads[index].at[:, first:first + deep], heads[index].at[:, last + 1:last + 1 + deep],
                 halo_send.at[step, 0], halo_recv.at[step, 1], tile(-1)),
            send(heads[index].at[:, last + 1 - deep:last + 1], heads[index].at[:, 0:deep],
                 halo_send.at[step, 1], halo_recv.at[step, 0], tile(1)),
        ]

    def top_halo(values, send_sem, recv_sem):
        depth = deep - 1
        return [
            send(values.at[first:first + depth], values.at[last + 1:last + 1 + depth],
                 send_sem.at[0], recv_sem.at[1], tile(-1)),
            send(values.at[last + 1 - depth:last + 1], values.at[first - depth:first],
                 send_sem.at[1], recv_sem.at[0], tile(1)),
        ]

    for copy in head_loads:
        copy.wait()
    beside += halo(0)
    for copy in recharge_loads:
        copy.wait()
    beside += top_halo(recharge, rain_send, rain_recv)

    loads["cell"].wait()
    loads["reach"].wait()
    loads["cond"].wait()
    live = reach[...] >= 0
    columns = jnp.where(live, cell[...], 0)
    reaches = jnp.where(live, reach[...], 0)
    for target_ref, values in (
            (weight, jnp.where(live, cond[...], 0.0)),
            (column_x, columns // width), (column_y, columns % width),
            (reach_high, reaches // LANES), (reach_low, reaches % LANES)):
        for bucket in range(buckets):
            for piece in range(pieces):
                line = bucket * pieces + piece
                target_ref[own(bucket), piece * LANES:(piece + 1) * LANES] = (
                    values[line:line + 1, :].astype(F32))

    def one_hot(ids, row):
        rows16 = jnp.broadcast_to(row, (16, slots)).astype(BF16)
        wide = jnp.concatenate([rows16] * (ids.shape[0] // 16), axis=0)
        return jnp.where(ids == wide, jnp.ones((), BF16), jnp.zeros((), BF16))

    ids = lax.broadcasted_iota(jnp.int32, (width, slots), 0)
    y_ids = ids.astype(F32).astype(BF16)
    x_ids = (ids // members).astype(F32).astype(BF16)
    r_ids = (ids % LANES).astype(F32).astype(BF16)
    flat = lax.broadcasted_iota(jnp.int32, (rows, slots), 0).astype(F32)
    total = jnp.zeros((2 * rows, width), F32)
    for bucket in range(buckets):
        wide = slot_range(bucket)
        values = one_hot(y_ids, column_y[own(bucket), :])
        one_y[:width, wide] = values
        one_y[width:, wide] = values
        terms = jnp.where(flat == column_x[own(bucket), :], weight[own(bucket), :], 0.0)
        total = total + dot_rows(jnp.concatenate(halves(terms), axis=0), one_y[:width, wide])
    total = total[:rows] + total[rows:]
    col_cond[first:last + 1, :] = total
    col_edge[...] = jnp.zeros(col_edge.shape, F32)
    col_edge[0, 0:deep - 1, :] = total[0:deep - 1]
    col_edge[1, 0:deep - 1, :] = total[rows - deep + 1:rows]
    beside += [
        send(col_edge.at[side], col_got.at[1 - side], col_send.at[side], col_recv.at[1 - side], tile(shift))
        for side, shift in ((0, -1), (1, 1))]
    for bucket in range(buckets):
        wide = slot_range(bucket)
        mask_x[:, wide] = one_hot(x_ids, column_x[own(bucket), :])
        one_r[:, wide] = one_hot(r_ids, reach_low[own(bucket), :])

    def unpack():
        for side in range(2):
            line = 0
            for target_ref, _, depth in packed:
                for layer in range(layers):
                    start = first - depth if side == 0 else last + 1
                    target_ref[layer, start:start + depth, :] = edge_got[side, line:line + depth, :]
                    line += depth
            start = first - deep + 1 if side == 0 else last + 1
            col_cond[start:start + deep - 1, :] = col_got[side, 0:deep - 1, :]

    def begin(block):
        for x in block:
            for layer in range(layers):
                term = capacity[layer, pl.ds(x, 1), :] * head0[layer, x]
                base[layer, x] = term + recharge[x] if layer == 0 else term

    lane = lax.broadcasted_iota(jnp.int32, (members, width), 1)

    def harmonic(first, second):
        return first * second / (first + second)

    def conduct(head, x):
        return tuple(
            kc[layer, pl.ds(x, 1), :]
            * jnp.exp(ka[layer, pl.ds(x, 1), :] * jnp.minimum(head[layer, x], 0.0))
            for layer in range(layers))

    def link_start(head):
        before_rows = conduct(head, 0)
        here = conduct(head, 1)
        before = tuple(harmonic(a, b) for a, b in zip(before_rows, here))
        for layer in range(layers):
            face_x[layer, 0] = before[layer]
        return here, before

    def link(head, start, stop, carry):
        size = 2

        def step(count, carry):
            here, before = carry
            for offset in range(size):
                x = start + count * size + offset
                after = conduct(head, x + 1)
                shut = ((x == first - 1) & (me == 0)) | ((x == last) & (me == tile_count - 1))
                inside = jnp.where(shut, 0.0, 1.0)
                ahead = tuple(inside * harmonic(a, b) for a, b in zip(here, after))
                down = None
                for layer in range(layers):
                    face_x[layer, x] = ahead[layer]
                    along = harmonic(here[layer], pltpu.roll(here[layer], width - 1, 1))
                    along = jnp.where(lane == width - 1, 0.0, along)
                    face_y[layer, x] = along
                    diagonal = capacity[layer, pl.ds(x, 1), :] + ahead[layer] + before[layer]
                    diagonal = diagonal + along + pltpu.roll(along, 1, 1)
                    if layer > 0:
                        diagonal = diagonal + down
                    if layer < layers - 1:
                        down = 0.5 * harmonic(here[layer], here[layer + 1])
                        face_z[layer, x] = down
                        diagonal = diagonal + down
                    if layer == 0:
                        diagonal = diagonal + col_cond[pl.ds(x, 1), :]
                    inverse[layer, x] = 1.0 / diagonal
                here, before = after, ahead
            return here, before

        return lax.fori_loop(0, (stop - start) // size, step, carry)

    def relax(head, x, which, with_river):
        now = {layer: head[layer, x] for layer in range(layers)
               if any(abs(layer - other) < 2 for other in which)}
        results = []
        for layer in which:
            along = face_y[layer, x]
            total = source[x] if layer == 0 and with_river else base[layer, x]
            total = total + face_x[layer, x] * head[layer, x + 1]
            total = total + face_x[layer, x - 1] * head[layer, x - 1]
            total = total + along * pltpu.roll(now[layer], width - 1, 1)
            total = total + pltpu.roll(along * now[layer], 1, 1)
            if layer < layers - 1:
                total = total + face_z[layer, x] * now[layer + 1]
            if layer > 0:
                total = total + face_z[layer - 1, x] * now[layer - 1]
            results.append(total * inverse[layer, x])
        return results

    every = list(range(layers))
    lower = every[1:]

    def sweep(index, which, with_river=True):
        def body(block):
            results = [relax(heads[index], x, which, with_river) for x in block]
            for x, result in zip(block, results):
                for layer, value in zip(which, result):
                    heads[index + 1][layer, x] = value
        return body

    def received(copies):
        for copy in copies:
            copy.wait_recv()

    def by_group(values):
        return jnp.concatenate([values[:, g * LANES:(g + 1) * LANES] for g in range(groups)], axis=0)

    def with_rate(rates, values):
        return jnp.concatenate(
            [rates[g:g + 1, :] * values[:, g * LANES:(g + 1) * LANES] for g in range(groups)], axis=1)

    def fetch(bucket, sections):
        left = jnp.concatenate(halves(by_group(sections)), axis=1)
        wide = slot_range(bucket)
        picked = jnp.dot(left, one_r[:, wide], preferred_element_type=F32)
        value = jnp.zeros((members, slots), F32)
        high = reach_high[own(bucket), :]
        for g in range(groups):
            value = value + jnp.where(high == g, picked[g * members:(g + 1) * members], 0.0)
        fetched[bucket] = value
        flow = weight[own(bucket), :] * value
        for part, term in enumerate(halves(jnp.concatenate([flow, flow], axis=0))):
            spread[part * rows * members:(part + 1) * rows * members, wide] = (
                mask_x[:, wide] * jnp.concatenate([term] * (rows // 2), axis=0))

    def river_sum(start, stop):
        wide = slice(start * slots, stop * slots)
        sums = dot_rows(spread[:, wide], one_y[:width, wide])
        return (sums[:rows * members] + sums[rows * members:]).reshape(rows, members, width)

    def top_terms(head):
        return jnp.concatenate(halves(head[0, first:last + 1].reshape(rows * members, width)), axis=1)

    def leak_part(terms, bucket, parts):
        wide = slot_range(bucket)
        picked = jnp.dot(terms, one_y[:, wide], preferred_element_type=F32)
        value = jnp.zeros((members, slots), F32)
        position = column_x[own(bucket), :]
        for x in range(rows):
            value = value + jnp.where(position == x, picked[x * members:(x + 1) * members], 0.0)
        flow = weight[own(bucket), :] * (fetched[bucket] - value)
        high = reach_high[own(bucket), :]
        split = jnp.concatenate([jnp.where(high == g, flow, 0.0) for g in range(groups)], axis=0)
        sums = dot_rows(jnp.concatenate(halves(split), axis=0), one_r[:LANES, wide])
        sums = sums[:groups * members] + sums[groups * members:]
        for g in range(groups):
            parts[bucket, :, g * LANES:(g + 1) * LANES] = sums[g * members:(g + 1) * members]

    def send_part(step, bucket, parts, got):
        return send(parts.at[bucket], got.at[bucket], leak_send.at[step, bucket],
                    leak_recv.at[step, bucket], owner(bucket))

    def near_leak(parts, got):
        values = parts[NEAR]
        for bucket in near:
            values = values + got[bucket]
        return values

    for bucket in [NEAR] + near:
        if bucket != NEAR:
            first_sections[bucket].wait_recv()
        fetch(bucket, section[...] if bucket == NEAR else sect0[bucket])
    received(beside)
    unpack()
    over(1, padded - 1, 2, begin)
    half = padded // 2
    carry = link(head0, 1, half, link_start(head0))
    first_sections[FAR].wait_recv()
    fetch(FAR, sect0[FAR])
    river0[first:last + 1] = river_sum(0, buckets)
    river_copies = top_halo(river0, river_send.at[0], river_recv.at[0])
    link(head0, half, padded - 1, carry)
    outer = [first - 2, first - 1, last + 1, last + 2]
    source[first:last + 1] = base[0, first:last + 1] + river0[first:last + 1]
    over(first, last + 1, 4, sweep(0, every))
    received(river_copies)
    for x in outer:
        source[x] = base[0, x] + river0[x]
    sweep(0, every)(outer[:2])
    sweep(0, every)(outer[2:])
    over(first - 1, last + 2, 2, sweep(1, every))

    over(first, last + 1, 4, sweep(2, every[:1]))
    terms = top_terms(head3)
    leak_part(terms, FAR, part1)
    copies = {FAR: send_part(0, FAR, part1, got1)}
    sweep(2, lower)(list(range(first, first + deep)))
    sweep(2, lower)(list(range(last + 1 - deep, last + 1)))
    halos = halo(SWEEPS)
    for bucket in near:
        leak_part(terms, bucket, part1)
        copies[bucket] = send_part(0, bucket, part1, got1)
    leak_part(terms, NEAR, part1)
    over(first + deep, last + 1 - deep, 2, sweep(2, lower))
    received(halos)
    carry = link(head3, 1, half, link_start(head3))

    loads["inflow"].wait()
    rate_copy.wait_recv()
    for bucket in near:
        copies[bucket].wait_recv()
    partial_state[...] = section[...] + with_rate(rate, inflow[...] - near_leak(part1, got1))
    state_copy = send(partial_state, state_got, state_send, state_recv, user(FAR))
    link(head3, half, padded - 1, carry)
    copies[FAR].wait_recv()
    sect1[NEAR] = partial_state[...] - with_rate(rate, got1[FAR])
    second_sections = {
        bucket: send(sect1.at[NEAR], sect1.at[bucket], sect_send.at[1, bucket], sect_recv.at[1, bucket], user(bucket))
        for bucket in near}

    over(1, padded - 1, 4, sweep(3, every, False))
    for bucket in [NEAR] + near:
        if bucket != NEAR:
            second_sections[bucket].wait_recv()
        fetch(bucket, sect1[bucket])
    river1[first:last + 1] = river_sum(0, FAR)
    state_copy.wait_recv()
    fetch(FAR, state_got[...] - with_rate(rate_got, part1[FAR]))
    river1[first:last + 1] = river1[first:last + 1] + river_sum(FAR, buckets)
    river_copies = top_halo(river1, river_send.at[1], river_recv.at[1])

    def add_river(block):
        for x in block:
            source[x] = base[0, x] + river1[x]
            head4[0, x] = head4[0, x] + river1[x] * inverse[0, x]

    over(first, last + 1, 4, add_river)
    over(first + 1, last, 3, sweep(4, every))
    over(first + 2, last - 1, 4, sweep(5, every))
    received(river_copies)
    add_river(outer)
    sweep(4, every)([first - 1, first])
    sweep(4, every)([last, last + 1])
    sweep(5, every[:1])([first, first + 1, last - 1, last])
    terms = top_terms(head6)
    leak_part(terms, FAR, part2)
    copies = {FAR: send_part(1, FAR, part2, got2)}
    for bucket in near:
        leak_part(terms, bucket, part2)
        copies[bucket] = send_part(1, bucket, part2, got2)
    leak_part(terms, NEAR, part2)
    sweep(5, lower)([first, first + 1])
    sweep(5, lower)([last - 1, last])
    stores = [pltpu.make_async_copy(head6.at[:, first:last + 1, m, :], head_out.at[m], store_sem.at[m])
              for m in range(members)]
    for copy in stores:
        copy.start()
    for bucket in near:
        copies[bucket].wait_recv()
    values = near_leak(part2, got2)
    copies[FAR].wait_recv()
    section_out[...] = section[...] + with_rate(rate, inflow[...] - (values + got2[FAR]))
    for copy in stores:
        copy.wait()
    for copy in sends:
        copy.wait_send()


def body(tile_count, head_start, recharge, section_start, inflow, soil_class, class_conduct, class_alpha,
         capacity, river_cell, river_reach, river_cond, reach_rate):
    members, layers, rows, width = head_start.shape
    buckets, slots = river_cell.shape[1:]
    lines = buckets * slots // LANES
    reaches = section_start.shape[1]
    groups = reaches // LANES
    any_spec = pl.BlockSpec(memory_space=pltpu.HBM)
    smem_spec = pl.BlockSpec(memory_space=pltpu.SMEM)
    vmem_spec = pl.BlockSpec(memory_space=pltpu.VMEM)
    vmem = pltpu.VMEM
    dma = pltpu.SemaphoreType.DMA
    padded = rows + 2 * SWEEPS
    lined = -(-padded // 8) * 8
    grid = (layers, padded, members, width)
    state = (members, reaches)
    every = buckets * slots
    package = layers * (3 * SWEEPS - 1)
    scratch = [vmem(grid, F32)] * (PICARD * SWEEPS + 1) + [
        vmem((padded, members, width), F32),
        vmem(state, F32), vmem(state, F32), vmem((layers, rows, width), jnp.int32), vmem((layers, rows, width), F32),
        vmem((lines, LANES), jnp.int32), vmem((lines, LANES), jnp.int32), vmem((lines, LANES), F32),
        vmem((groups, LANES), F32),
        vmem((layers, lined, width), F32), vmem((layers, lined, width), F32), vmem((layers, lined, width), F32),
        vmem(grid, F32), vmem((padded, members, width), F32),
        vmem(grid, F32), vmem(grid, F32), vmem((layers - 1,) + grid[1:], F32), vmem(grid, F32),
        vmem((lined, width), F32), vmem((padded, members, width), F32), vmem((padded, members, width), F32),
        vmem((2 * width, every), BF16), vmem((rows * members, every), BF16), vmem((2 * LANES, every), BF16),
        vmem((2 * rows * members, every), BF16),
    ] + [vmem((buckets, slots), F32)] * 5 + [
        vmem((buckets, members, slots), F32),
        vmem((2, package, width), F32), vmem((2, package, width), F32),
        vmem((2, 8, width), F32), vmem((2, 8, width), F32),
    ] + [vmem((buckets,) + state, F32)] * 6 + [vmem(state, F32)] * 2 + [vmem((groups, LANES), F32)] + [
        dma((8,)), dma((members,)), dma((members,)), dma((members,)),
        dma((PICARD, 2)), dma((PICARD, 2)), dma((2,)), dma((2,)),
        dma((2,)), dma((2,)), dma((2,)), dma((2,)), dma((PICARD, 2)), dma((PICARD, 2)),
        dma((2, buckets)), dma((2, buckets)), dma((2, buckets)), dma((2, buckets)),
        dma, dma, dma, dma,
    ]
    return pl.pallas_call(
        functools.partial(kernel, tile_count),
        out_shape=(vmem(head_start.shape, F32), vmem(state, F32)),
        in_specs=[any_spec] * 5 + [smem_spec] * 2 + [any_spec] * 5,
        out_specs=(vmem_spec, vmem_spec),
        scratch_shapes=scratch,
        compiler_params=pltpu.CompilerParams(
            collective_id=0, has_side_effects=True, vmem_limit_bytes=62 * 1024 * 1024),
        name="aquifer",
    )(head_start, recharge, section_start, inflow, soil_class, class_conduct, class_alpha, capacity,
      river_cell.reshape(lines, LANES), river_reach.reshape(lines, LANES), river_cond.reshape(lines, LANES),
      reach_rate.reshape(groups, LANES))


def solution(mesh):
    return jax.shard_map(
        functools.partial(body, mesh.shape["space"]),
        mesh=mesh,
        in_specs=(
            P("member", None, "space", None),
            P("member", "space", None),
            P("member", "space"),
            P("member", "space"),
            P(None, "space", None),
            P(),
            P(),
            P(None, "space", None),
            P("space", None, None),
            P("space", None, None),
            P("space", None, None),
            P("space"),
        ),
        out_specs=(P("member", None, "space", None), P("member", "space")),
        check_vma=False,
    )
```
